128 devices in a mesh: head: 4 (over y), tok: 32 (over x, z, core).
Axes of the slice: x: 4, y: 4, z: 4, core: 2. Of those that a mesh axis runs over, the one named last changes fastest.
Arguments:
- tokens: bfloat16 [8192, 2048], P(('tok', 'head')), may hold values from -6 to 6
- token_req: int32 [8192], P(('tok', 'head')), may hold values from 0 to 1, as said below
- cache_len: int32 [64], P('tok'), may hold values from 16 to 1023, as said below
- sink_count: int32 [64], P('tok'), may hold values from 1 to 8
- cache_k: bfloat16 [64, 1024, 2048], P('tok', None, 'head'), may hold values from -64 to 64
- cache_v: bfloat16 [64, 1024, 2048], P('tok', None, 'head'), may hold values from -6 to 6
- attn_gain: float32 [2048], replicated, may hold values from 0.1 to 1.9
- w_qkv: bfloat16 [2048, 3, 2048], P(None, None, 'head'), may hold values from -0.125 to 0.125
- w_out: bfloat16 [2048, 2048], P('head'), may hold values from -0.125 to 0.125
- ffn_gain: float32 [2048], replicated, may hold values from 0.1 to 1.9
- routes: int32 [8192, 8], P(('tok', 'head')), may hold values from 0 to 63, all different within a row; in each aligned block of 64 rows (0 to 63, 64 to 127, ...) at most 16 rows name the same one
- route_weight: float32 [8192, 8], P(('tok', 'head')), may hold values from 0.1 to 1
- w_expert: bfloat16 [64, 3, 2048, 1024], P('tok', None, None, 'head'), may hold values from -0.125 to 0.125
Outputs:
- hidden_out: bfloat16 [8192, 2048], P(('tok', 'head'))
- new_cache_k: bfloat16 [64, 1024, 2048], P('tok', None, 'head')
- new_cache_v: bfloat16 [64, 1024, 2048], P('tok', None, 'head')
The draws below stay inside these ranges and needn't reach their ends.
Inputs may be any that keep to these rules, and one draw needn't show every extreme that they name: `token_req`: within each group of 256 consecutive tokens, the tokens of request 0 come first and those of request 1 follow; each request has at least one token. `cache_len`: A request's cache length plus its number of tokens is at most 1024. `routes`: each row names 8 different experts; in each aligned block of 64 rows (the rows of one device) no expert is named more than 16 times.
All inputs are finite; a program needn't handle non-finite values.
Results may differ from the reference program's by a relative error of at most 0.018.
Values may be sent and summed in bfloat16 or wider, within the bound.
No kernel may reach another device: no remote copies, remote signals or barrier semaphores. Data moves between devices by JAX's collectives and lax.ppermute only.
A program may use at most 192 MiB of HBM per device.

```python
import math
import jax
import jax.numpy as jnp
import numpy as np
from jax import lax

D = 2048
H = 16
HD = 128
FF = 1024
TOPK = 8
TOK_DEV = 64
REQ_GRP = 2
CAP = 1024
WIN = 384
EXPERTS = 64
TOK_GRP = 256
TOKENS = 8192
REQS = 64
MOST = 16


def layout_parts(key):
    folded = jax.random.fold_in(key, 11)
    groups = TOKENS // TOK_GRP
    key_one, key_two, key_three, key_four, key_five = jax.random.split(folded, 5)
    single = jax.random.randint(key_one, (groups,), 0, 2).at[0].set(1)
    sizeable = jax.random.randint(key_two, (groups,), TOK_GRP // 4, TOK_GRP // 2 + 1)
    second_count = jnp.where(single == 1, 1, sizeable)
    first_count = TOK_GRP - second_count
    counts = jnp.stack([first_count, second_count], axis=1)
    position = jnp.arange(TOK_GRP, dtype=jnp.int32)
    request = (position[None, :] >= first_count[:, None]).astype(jnp.int32).reshape(-1)
    long_flag = jax.random.randint(key_three, (groups, 2), 0, 2).at[0, 0].set(1).at[0, 1].set(1).at[groups - 1, 0].set(0)
    offset = jax.random.randint(key_four, (groups, 2), 0, CAP // 16).at[0, 0].set(0).at[0, 1].set(0)
    short_len = jax.random.randint(key_five, (groups, 2), 16, CAP // 8).at[groups - 1, 0].set(16)
    lengths = jnp.where(long_flag == 1, CAP - counts - offset, short_len)
    return (request, lengths.reshape(-1).astype(jnp.int32))


def draw_token_req(key, part):
    return layout_parts(key)[0]


def draw_cache_len(key, part):
    return layout_parts(key)[1]


def draw_cache_k(key, part):
    full_shape = (REQS, CAP, H * HD)
    values = jax.random.normal(key, full_shape, jnp.float32) * 2.0
    return jnp.clip(values, -64.0, 64.0).astype(jnp.bfloat16)


def place_ends(result, key, least, largest):
    extent = result.shape
    index_at = [jax.random.randint(jax.random.fold_in(key, axis), (), 0, extent[axis]) for axis in range(len(extent))]
    result = result.at[tuple(index_at)].set(least)
    longest = extent.index(max(extent))
    index_at[longest] = (index_at[longest] + 1) % extent[longest]
    return result.at[tuple(index_at)].set(largest)


def block_levels(own_key, extent, cuts, least, high):
    level = 1.0
    for dim, shards_of in cuts:
        steps = jax.random.uniform(jax.random.fold_in(jax.random.fold_in(own_key, 6), dim), (shards_of,), jnp.float32, least / len(cuts), high / len(cuts))
        level = level * jnp.repeat(jnp.exp(steps), extent[dim] // shards_of).reshape((-1,) + (1,) * (len(extent) - 1 - dim))
    return level


def shared_out(key, own, number, rows, number_of, top, most, lean):
    sequence = jax.random.permutation(key, number_of)
    packed, usual = portions_of(number_of, rows * top, most, lean, True), portions_of(number_of, rows * top, most, lean, False)
    places = jnp.arange(number_of)

    def named(sizes, offset_by):
        used = int((sizes > 0).sum())
        fixed = max(1, used // 4)
        shifted = fixed + (places - fixed + offset_by * (used - fixed)) % max(1, number_of - fixed)
        return jnp.zeros((number_of,), jnp.int32).at[sequence[jnp.where(places < fixed, places, shifted)]].set(jnp.asarray(sizes, jnp.int32))

    sizes = jnp.where(number % 4 == 0, named(packed, number // 4), named(usual, number - number // 4 - 1))
    mixed = jax.random.permutation(jax.random.fold_in(own, 3), number_of)
    donor, taker = mixed[0:number_of // 2 * 2:2], mixed[1:number_of // 2 * 2:2]
    margin = jnp.minimum(sizes[donor] - 1, most - sizes[taker]) // 2
    margin = jnp.where((donor == sequence[0]) | (taker == sequence[0]) | (sizes[taker] == 0), 0, jnp.maximum(margin, 0))
    shifted = jax.random.randint(jax.random.fold_in(own, 4), (number_of // 2,), 0, 1 << 20) % (margin + 1)
    sizes = sizes.at[donor].add(-shifted).at[taker].add(shifted)
    items = jnp.searchsorted(jnp.cumsum(sizes), jnp.arange(rows * top), side="right").astype(jnp.int32)
    grid = items.reshape(top, rows).T
    grid = grid[jax.random.permutation(jax.random.fold_in(own, 1), rows)]
    offset_by = jax.random.randint(jax.random.fold_in(own, 2), (rows, 1), 0, top)
    return jnp.take_along_axis(grid, (jnp.arange(top)[None, :] + offset_by) % top, axis=1)


def portions_of(amount, total, most, skew, full):
    weights = [(1 << 20) // math.isqrt(rank ** skew) + 1 for rank in range(1, amount + 1)]
    largest = most if full else min(most, max(-(-total // amount), total * weights[0] // sum(weights)))
    least = 1 if total - largest >= amount - 1 else 0
    given, rest = [largest] + [least] * (amount - 1), total - largest - least * (amount - 1)
    while rest > 0:
        candidates = [i for i in range(1, amount) if given[i] < largest] or [i for i in range(1, amount) if given[i] < most]
        pool, budget = sum([weights[i] for i in candidates]), rest
        for i in candidates:
            extra = min(most - given[i], max(1, budget * weights[i] // pool), rest)
            given[i] = given[i] + extra
            rest = rest - extra
    return np.array(given)


def centred(key, dims, scale, most, pieces=(), kind=jnp.bfloat16):
    result = jax.random.normal(key, dims, jnp.float32) * scale
    if len(pieces) > 0:
        result = block_levels(key, dims, pieces, -0.22, 0.18) * result
    return jnp.clip(result, min=-most, max=most).astype(kind)


def setup_inputs(seed: int = 0) -> dict:
    splits = jax.random.split(jax.random.key(seed), 14)
    tokens = centred(splits[0], (TOKENS, D), 1.0, 6.0, ((0, 128),))
    token_req = draw_token_req(jax.random.fold_in(splits[13], 71), 0)
    cache_len = draw_cache_len(jax.random.fold_in(splits[13], 71), 0)
    sink_count = place_ends(jax.random.randint(splits[3], (REQS,), 1, 9), jax.random.fold_in(splits[3], 1), 1, 8).astype(jnp.int32)
    cache_k = draw_cache_k(jax.random.fold_in(splits[13], 71), 0)
    cache_v = centred(splits[5], (REQS, CAP, H * HD), 1.0, 6.0, ((0, 32), (2, 4)))
    attn_gain = jnp.clip(1.0 + 0.18 * jax.random.normal(splits[6], (D,), jnp.float32), 0.1, 1.9)
    w_qkv = centred(splits[7], (D, 3, H * HD), D ** -0.5, 0.125, ((2, 4),))
    w_out = centred(splits[8], (H * HD, D), (H * HD) ** -0.5, 0.125, ((0, 4),))
    ffn_gain = jnp.clip(1.0 + 0.18 * jax.random.normal(splits[9], (D,), jnp.float32), 0.1, 1.9)
    routes_keys = jax.random.split(jax.random.fold_in(splits[10], 1), TOKENS // TOK_DEV)
    routes_turns = jax.random.permutation(jax.random.fold_in(splits[10], 3), TOKENS // TOK_DEV)
    routes = jax.vmap(lambda own, number: shared_out(jax.random.fold_in(splits[10], 2), own, number, TOK_DEV, EXPERTS, TOPK, MOST, 2))(routes_keys, routes_turns).reshape((TOKENS, TOPK))
    route_weight = jnp.clip(jnp.exp(math.log(1.0) - 2.3025851 * jax.random.uniform(splits[11], (TOKENS, TOPK), jnp.float32) ** block_levels(splits[11], (TOKENS, TOPK), ((0, 128),), -0.2, 0.2)), 0.1, 1.0)
    w_expert = centred(splits[12], (EXPERTS, 3, D, FF), D ** -0.5, 0.125, ((0, 32), (3, 4)))
    return {"tokens": tokens, "token_req": token_req, "cache_len": cache_len, "sink_count": sink_count, "cache_k": cache_k, "cache_v": cache_v, "attn_gain": attn_gain, "w_qkv": w_qkv, "w_out": w_out, "ffn_gain": ffn_gain, "routes": routes, "route_weight": route_weight, "w_expert": w_expert}


norm_eps = 1e-05
rope_base = 50000.0

def rms_norm(values, gain_vec):
    widened = values.astype(jnp.float32)
    return widened * lax.rsqrt(lax.optimization_barrier(jnp.mean(widened * widened, axis=-1, keepdims=True)) + norm_eps) * gain_vec

def rotate(vectors, positions_all):
    half_width = vectors.shape[-1] // 2
    frequency = rope_base ** (-(jnp.arange(half_width, dtype=jnp.float32) * 2.0 / vectors.shape[-1]))
    angles = positions_all.astype(jnp.float32)[:, None] * frequency[None, :]
    cosine = jnp.cos(angles)[:, None, :]
    sine_part = jnp.sin(angles)[:, None, :]
    first_half = vectors[..., :half_width]
    second_half = vectors[..., half_width:]
    return jnp.concatenate([first_half * cosine - second_half * sine_part, second_half * cosine + first_half * sine_part], axis=-1)

def positions(request, lengths):
    one_hot = (request[:, None] == jnp.arange(REQ_GRP, dtype=jnp.int32)[None, :]).astype(jnp.int32)
    before = jnp.cumsum(one_hot, axis=0) - one_hot
    return lax.optimization_barrier(jnp.sum(one_hot * (before + lengths[None, :]), axis=1)).astype(jnp.int32)

def attend(query, keys_all, values_all, request, positions_all, sink_counts):
    scores = jnp.einsum('thd,rjhd->thrj', query.astype(jnp.float32), keys_all.astype(jnp.float32)) * HD ** (-0.5)
    slot_ids = jnp.arange(CAP, dtype=jnp.int32)
    same_req = jnp.arange(REQ_GRP, dtype=jnp.int32)[None, :, None] == request[:, None, None]
    causal = slot_ids[None, None, :] <= positions_all[:, None, None]
    window = (slot_ids[None, None, :] < sink_counts[None, :, None]) | (slot_ids[None, None, :] > positions_all[:, None, None] - WIN)
    allowed = (same_req & causal & window)[:, None]
    masked = jnp.where(allowed, scores, -1e+30)
    row_max = lax.optimization_barrier(jnp.max(masked, axis=(2, 3), keepdims=True))
    exp_scores = jnp.exp(masked - row_max)
    weights = (exp_scores / lax.optimization_barrier(jnp.sum(exp_scores, axis=(2, 3), keepdims=True))).astype(jnp.bfloat16)
    return jnp.einsum('thrj,rjhd->thd', weights.astype(jnp.float32), values_all.astype(jnp.float32)).astype(jnp.bfloat16)

def reference(tokens, token_req, cache_len, sink_count, cache_k, cache_v, attn_gain, w_qkv, w_out, ffn_gain, routes, route_weight, w_expert):
    groups = TOKENS // TOK_GRP
    normed = rms_norm(tokens, attn_gain).astype(jnp.bfloat16)
    projected = jnp.dot(normed, w_qkv.reshape(D, 3 * H * HD), preferred_element_type=jnp.float32).reshape(TOKENS, 3, H, HD)
    req_groups = token_req.reshape(groups, TOK_GRP)
    positions_all = jax.vmap(positions)(req_groups, cache_len.reshape(groups, REQ_GRP)).reshape(TOKENS)
    query = rotate(projected[:, 0], positions_all).astype(jnp.bfloat16)
    key_new = rotate(projected[:, 1], positions_all).astype(jnp.bfloat16).reshape(TOKENS, H * HD)
    value_new = projected[:, 2].astype(jnp.bfloat16).reshape(TOKENS, H * HD)
    owner_row = jnp.arange(TOKENS, dtype=jnp.int32) // TOK_GRP * REQ_GRP + token_req
    new_cache_k = cache_k.at[owner_row, positions_all].set(key_new)
    new_cache_v = cache_v.at[owner_row, positions_all].set(value_new)

    def one_group(group_args):
        group_query, group_keys, group_values, group_req, group_pos, group_sinks = group_args
        return attend(group_query, group_keys.reshape(REQ_GRP, CAP, H, HD), group_values.reshape(REQ_GRP, CAP, H, HD), group_req, group_pos, group_sinks)
    attended = lax.map(one_group, (query.reshape(groups, TOK_GRP, H, HD), new_cache_k.reshape(groups, REQ_GRP, CAP, H * HD), new_cache_v.reshape(groups, REQ_GRP, CAP, H * HD), req_groups, positions_all.reshape(groups, TOK_GRP), sink_count.reshape(groups, REQ_GRP)))
    attended = attended.reshape(TOKENS, H * HD)
    residual = (tokens.astype(jnp.float32) + jnp.dot(attended, w_out, preferred_element_type=jnp.float32)).astype(jnp.bfloat16)
    ffn_input = rms_norm(residual, ffn_gain).astype(jnp.bfloat16)
    device_count = TOKENS // TOK_DEV
    flat_expert = routes.reshape(-1).astype(jnp.int32)
    one_hot = (flat_expert[:, None] == jnp.arange(EXPERTS, dtype=jnp.int32)[None, :]).astype(jnp.int32)
    one_hot = one_hot.reshape(device_count, TOK_DEV * TOPK, EXPERTS)
    before = jnp.cumsum(one_hot, axis=1) - one_hot
    slot_index = lax.optimization_barrier(jnp.sum(before * one_hot, axis=2)).reshape(-1).astype(jnp.int32)
    row_ids = jnp.arange(TOKENS * TOPK, dtype=jnp.int32)
    device_of = row_ids // (TOK_DEV * TOPK)
    token_of = row_ids // TOPK
    slot_table = jnp.full((EXPERTS, device_count, MOST), TOKENS, jnp.int32).at[flat_expert, device_of, slot_index].set(token_of)
    padded = jnp.concatenate([ffn_input, jnp.zeros((1, D), jnp.bfloat16)], axis=0)

    def one_expert(expert_args):
        table_rows, weight_set = expert_args
        slot_rows = padded[table_rows]
        gate_part = jnp.dot(slot_rows, weight_set[0], preferred_element_type=jnp.float32)
        up_part = jnp.dot(slot_rows, weight_set[1], preferred_element_type=jnp.float32)
        hidden = (jax.nn.silu(gate_part) * up_part).astype(jnp.bfloat16)
        return lax.dot_general(hidden, weight_set[2], (((1,), (1,)), ((), ())), preferred_element_type=jnp.float32).astype(jnp.bfloat16)
    expert_out = lax.map(one_expert, (slot_table.reshape(EXPERTS, device_count * MOST), w_expert))
    picked = expert_out.reshape(-1, D)[flat_expert * (device_count * MOST) + device_of * MOST + slot_index]
    combined = lax.optimization_barrier(jnp.sum(route_weight.reshape(TOKENS, TOPK, 1) * picked.reshape(TOKENS, TOPK, D).astype(jnp.float32), axis=1))
    hidden_out = (residual.astype(jnp.float32) + combined).astype(jnp.bfloat16)
    return (hidden_out, new_cache_k, new_cache_v)
```

```python
import functools
import math

import jax
import jax.numpy as jnp
from jax import lax
from jax.experimental import pallas as pl
from jax.experimental.pallas import tpu as pltpu
from jax.sharding import PartitionSpec as P

HD = 128
WIN = 384
MOST = 16
norm_eps = 1e-05
rope_base = 50000.0
NX, NZ, NY = 4, 4, 4
BF = jnp.bfloat16
F32 = jnp.float32
TAIL = 128


def tok_perm(move):
    pairs = []
    for x in range(NX):
        for z in range(NZ):
            for c in range(2):
                nx, nz, nc = move(x, z, c)
                pairs.append(((x * NZ + z) * 2 + c, ((nx % NX) * NZ + nz % NZ) * 2 + nc))
    return pairs


def shift(value, axis, step):
    if axis == "y":
        return lax.ppermute(value, "head", [(i, (i + step) % NY) for i in range(NY)])
    if axis == "x":
        return lax.ppermute(value, "tok", tok_perm(lambda x, z, c: (x + step, z, c)))
    return lax.ppermute(value, "tok", tok_perm(lambda x, z, c: (x, z + step, c)))


def swap_core(value):
    return lax.ppermute(value, "tok", tok_perm(lambda x, z, c: (x, z, 1 - c)))


def ring_gather(value, axis):
    half = value.shape[0] // 2
    left = shift(value, axis, 1)
    right = shift(value, axis, -1)
    far_a = shift(left[:half], axis, 1)
    far_b = shift(right[half:], axis, -1)
    return value, left, right, far_a, far_b


def ring_scatter(own, left, right, far_a, far_b, axis):
    got_a = shift(far_a, axis, 1)
    got_b = shift(far_b, axis, -1)
    half = far_a.shape[0]
    right = right.astype(F32)
    left = left.astype(F32)
    to_right = jnp.concatenate([right[:half] + got_a.astype(F32), right[half:]], axis=0)
    to_left = jnp.concatenate([left[:half], left[half:] + got_b.astype(F32)], axis=0)
    from_left = shift(to_right.astype(BF), axis, 1)
    from_right = shift(to_left.astype(BF), axis, -1)
    return own.astype(F32) + from_left.astype(F32) + from_right.astype(F32)


def nt_dot(a, b):
    return lax.dot_general(a, b, (((1,), (1,)), ((), ())), preferred_element_type=F32)


def attn_kernel(
    info,
    x0,
    x1,
    x2,
    x3,
    x4,
    gain,
    w3,
    cos,
    sin,
    ck,
    cv,
    wo,
    nk,
    nv,
    m0,
    m1,
    m2,
    m3,
    m4,
    xn,
    hot,
    bias,
    att,
    *,
    rows,
    heads,
    cap,
):
    h = pl.program_id(0)
    count0, len0, len1, sink0, sink1 = info[0], info[1], info[2], info[3], info[4]
    part = rows // 4

    def index_of(iota):
        piece = iota // part
        base = jnp.where(
            piece == 0,
            info[5],
            jnp.where(piece == 1, info[6], jnp.where(piece == 2, info[7], info[8])),
        )
        return base + iota % part

    col = index_of(lax.broadcasted_iota(jnp.int32, (rows, 1), 0))
    first_col = col < count0
    pos_col = jnp.where(first_col, len0 + col, len1 + col - count0)

    @pl.when(h == 0)
    def _():
        xs = jnp.concatenate([x0[...], x1[...], x2[...], x3[...], x4[...]], axis=0).astype(F32)
        mean = jnp.mean(xs * xs, axis=-1, keepdims=True)
        xn[...] = (xs * lax.rsqrt(mean + norm_eps) * gain[...]).astype(BF)
        row = index_of(lax.broadcasted_iota(jnp.int32, (1, rows), 1))
        first_row = row < count0
        slot_row = jnp.where(first_row, len0 + row, cap + len1 + row - count0)
        slots = lax.broadcasted_iota(jnp.int32, (2 * cap, rows), 0)
        hot[...] = (slots == slot_row).astype(F32).astype(BF)
        j = lax.broadcasted_iota(jnp.int32, (rows, cap), 1)
        sinks = jnp.where(first_col, sink0, sink1)
        ok = (j <= pos_col) & ((j < sinks) | (j > pos_col - WIN))
        bias[...] = jnp.where(ok, 0.0, -1e30)

    xv = xn[...]
    q = jnp.dot(xv, w3[0], preferred_element_type=F32)
    k = jnp.dot(xv, w3[1], preferred_element_type=F32)
    v = jnp.dot(xv, w3[2], preferred_element_type=F32)
    c, s = cos[...], sin[...]
    q = (q * c + pltpu.roll(q, HD // 2, 1) * s).astype(BF)
    k = (k * c + pltpu.roll(k, HD // 2, 1) * s).astype(BF)
    kv = jnp.concatenate([k, v.astype(BF)], axis=1)
    slot = lax.broadcasted_iota(jnp.int32, (cap, 1), 0)
    scale = HD**-0.5
    scores = []
    values = []
    for r, start, number in ((0, len0, count0), (1, len1, rows - count0)):
        ins = jnp.dot(hot[r * cap : (r + 1) * cap, :], kv, preferred_element_type=F32)
        fresh = (slot >= start) & (slot < start + number)
        new_k = jnp.where(fresh, ins[:, :HD], ck[r].astype(F32)).astype(BF)
        new_v = jnp.where(fresh, ins[:, HD:], cv[r].astype(F32)).astype(BF)
        nk[r] = new_k
        nv[r] = new_v
        scores.append(nt_dot(q, new_k))
        values.append(new_v)
    masked = jnp.where(first_col, scores[0], scores[1]) * scale + bias[...]
    top = jnp.max(masked, axis=1, keepdims=True)
    weights = jnp.exp(masked - top)
    total = jnp.sum(weights, axis=1, keepdims=True)
    w0 = jnp.where(first_col, weights, 0.0).astype(BF)
    w1 = jnp.where(first_col, 0.0, weights).astype(BF)
    out = jnp.dot(w0, values[0], preferred_element_type=F32) + jnp.dot(
        w1, values[1], preferred_element_type=F32
    )
    att[h] = (out / total).astype(BF)

    @pl.when(h == heads - 1)
    def _():
        both = jnp.concatenate([att[i] for i in range(heads)], axis=1)
        mixed = jnp.dot(both, wo[...], preferred_element_type=F32).astype(BF)
        m0[...] = mixed[:part]
        m1[...] = mixed[part : 2 * part]
        m2[...] = mixed[2 * part : 3 * part]
        m3[...] = mixed[3 * part : 3 * part + part // 2]
        m4[...] = mixed[3 * part + part // 2 :]


def attention(info, pieces, gain, w3, cos, sin, cache_k, cache_v, w_out):
    part, width = pieces[0].shape
    rows = 4 * part
    reqs, cap, cols = cache_k.shape
    heads = cols // HD
    fixed = lambda *shape: pl.BlockSpec(shape, lambda h, i: (0,) * len(shape))
    x_specs = [fixed(*p.shape) for p in pieces]
    cache_spec = pl.BlockSpec((reqs, cap, HD), lambda h, i: (0, 0, h))
    outs = [jax.ShapeDtypeStruct(cache_k.shape, BF)] * 2 + [
        jax.ShapeDtypeStruct(p.shape, BF) for p in pieces
    ]
    return pl.pallas_call(
        functools.partial(attn_kernel, rows=rows, heads=heads, cap=cap),
        out_shape=outs,
        grid_spec=pltpu.PrefetchScalarGridSpec(
            num_scalar_prefetch=1,
            grid=(heads,),
            in_specs=x_specs
            + [
                fixed(1, width),
                pl.BlockSpec((3, width, HD), lambda h, i: (0, 0, h)),
                fixed(rows, HD),
                fixed(rows, HD),
                cache_spec,
                cache_spec,
                fixed(*w_out.shape),
            ],
            out_specs=[cache_spec, cache_spec] + x_specs,
            scratch_shapes=[
                pltpu.VMEM((rows, width), BF),
                pltpu.VMEM((2 * cap, rows), BF),
                pltpu.VMEM((rows, cap), F32),
                pltpu.VMEM((heads, rows, HD), BF),
            ],
        ),
        compiler_params=pltpu.CompilerParams(vmem_limit_bytes=56 << 20),
        name="attn",
    )(info, *pieces, gain, w3, cos, sin, cache_k, cache_v, w_out)


def expert_kernel(ids, *refs, plan, tiles, block):
    n = len(plan)
    xs = refs[:n]
    w_own, w_oth, wy0, wy1, wz0, wz1 = refs[n : n + 6]
    outs = refs[n + 6 : 2 * n + 6]
    xt, wt, xg, yt, mix, sem_x, sem_w, sem_o = refs[2 * n + 6 :]
    rows = xt.shape[1]
    width = yt.shape[2]
    blocks = rows // block
    lot = blocks * MOST
    slots = 4 * lot

    loads = []
    for i, (tile, at) in enumerate(plan):
        size = xs[i].shape[0]
        loads.append(
            pltpu.make_async_copy(xs[i], xt.at[tile, pl.ds(at, size)], sem_x.at[i])
        )
        loads[-1].start()
    sources = [
        (w_own.at[0], wy0),
        (w_own.at[1], wy1),
        (w_oth.at[0], wz0),
        (w_oth.at[1], wz1),
    ]
    weights = []
    for e in range(4):
        pair = []
        for s in range(2):
            copy = pltpu.make_async_copy(sources[e][s], wt.at[e, s], sem_w.at[e, s])
            copy.start()
            pair.append(copy)
        weights.append(pair)

    lane = lax.broadcasted_iota(jnp.int32, (TAIL, slots), 0)
    column = lax.broadcasted_iota(jnp.int32, (TAIL, slots), 1)
    which = column // lot
    wanted = jnp.where(
        which == 0, ids[0], jnp.where(which == 1, ids[1], jnp.where(which == 2, ids[2], ids[3]))
    )
    spread = (lane == wanted).astype(F32).astype(BF)
    ti = lax.broadcasted_iota(jnp.int32, (rows, rows), 0)
    tj = lax.broadcasted_iota(jnp.int32, (rows, rows), 1)
    earlier = ((tj < ti) & (ti // block == tj // block)).astype(F32).astype(BF)
    sc = lax.broadcasted_iota(jnp.int32, (rows, slots), 1)
    st = lax.broadcasted_iota(jnp.int32, (rows, slots), 0)
    same_block = (sc // MOST) % blocks == st // block
    slot_of = (sc % MOST).astype(F32)

    for t in range(tiles):
        for i, (tile, _) in enumerate(plan):
            if tile == t:
                loads[i].wait()
        share = jnp.dot(xt[t, :, width:], spread, preferred_element_type=F32)
        taken = (share > 0.0).astype(F32)
        before = jnp.dot(earlier, taken.astype(BF), preferred_element_type=F32)
        here = same_block & (before == slot_of) & (share > 0.0)
        mix[t] = jnp.where(here, share, 0.0).astype(BF)
        picks = here.astype(F32).astype(BF)
        got = lax.dot_general(
            picks, xt[t, :, :width], (((0,), (0,)), ((), ())), preferred_element_type=F32
        ).astype(BF)
        for e in range(4):
            xg[e, t * lot : (t + 1) * lot, :] = got[e * lot : (e + 1) * lot]

    for e in range(4):
        x = xg[e]
        acts = []
        for s in range(2):
            weights[e][s].wait()
            gate = jnp.dot(x, wt[e, s, 0], preferred_element_type=F32)
            up = jnp.dot(x, wt[e, s, 1], preferred_element_type=F32)
            acts.append((gate / (1.0 + jnp.exp(-gate)) * up).astype(BF))
        step = 512 if width % 512 == 0 else width
        for d in range(0, width, step):
            part = nt_dot(acts[0], wt[e, 0, 2, d : d + step, :]) + nt_dot(
                acts[1], wt[e, 1, 2, d : d + step, :]
            )
            part = part.astype(BF)
            for t in range(tiles):
                yt[t, e * lot : (e + 1) * lot, d : d + step] = part[t * lot : (t + 1) * lot]

    stores = []
    for t in range(tiles):
        xt[t, :, :width] = jnp.dot(mix[t], yt[t], preferred_element_type=F32).astype(BF)
        for i, (tile, at) in enumerate(plan):
            if tile == t:
                size = outs[i].shape[0]
                copy = pltpu.make_async_copy(
                    xt.at[t, pl.ds(at, size), pl.ds(0, width)], outs[i], sem_o.at[i]
                )
                copy.start()
                stores.append(copy)
    for copy in stores:
        copy.wait()


def experts(ids, pieces, weights, rows, block, name):
    plan = []
    at = 0
    for p in pieces:
        plan.append((at // rows, at % rows))
        at += p.shape[0]
    tiles = at // rows
    wide = pieces[0].shape[1]
    width = wide - TAIL
    lot = rows // block * MOST
    n = len(pieces)
    any_spec = pl.BlockSpec(memory_space=pl.ANY)
    ff = weights[0].shape[-1]
    return pl.pallas_call(
        functools.partial(expert_kernel, plan=tuple(plan), tiles=tiles, block=block),
        out_shape=[jax.ShapeDtypeStruct((p.shape[0], width), BF) for p in pieces],
        in_specs=[pl.BlockSpec(memory_space=pltpu.SMEM)] + [any_spec] * (n + 6),
        out_specs=[any_spec] * n,
        scratch_shapes=[
            pltpu.VMEM((tiles, rows, wide), BF),
            pltpu.VMEM((4, 2, 3, width, ff), BF),
            pltpu.VMEM((4, tiles * lot, width), BF),
            pltpu.VMEM((tiles, 4 * lot, width), BF),
            pltpu.VMEM((tiles, rows, 4 * lot), BF),
            pltpu.SemaphoreType.DMA((n,)),
            pltpu.SemaphoreType.DMA((4, 2)),
            pltpu.SemaphoreType.DMA((n,)),
        ],
        compiler_params=pltpu.CompilerParams(vmem_limit_bytes=60 << 20),
        name=name,
    )(ids, *pieces, *weights)


def on_device(
    tokens,
    token_req,
    cache_len,
    sink_count,
    cache_k,
    cache_v,
    attn_gain,
    w_qkv,
    w_out,
    ffn_gain,
    routes,
    route_weight,
    w_expert,
):
    part, width = tokens.shape
    y = lax.axis_index("head")
    tok = lax.axis_index("tok")

    own, left, right, far_a, far_b = ring_gather(tokens, "y")
    zeros_here = jnp.full((8, 128), jnp.sum((token_req == 0).astype(jnp.int32)), jnp.int32)
    count0 = (
        zeros_here + shift(zeros_here, "y", 1) + shift(zeros_here, "y", -1) + shift(zeros_here, "y", 2)
    )[0, 0]
    base = (jnp.stack([y, y + 3, y + 1, y + 2]) % NY * part).astype(jnp.int32)
    index = (base[:, None] + jnp.arange(part, dtype=jnp.int32)[None, :]).reshape(-1)
    position = jnp.where(index < count0, cache_len[0] + index, cache_len[1] + index - count0)
    frequency = rope_base ** (-(jnp.arange(HD // 2, dtype=F32) * 2.0 / HD))
    angles = position.astype(F32)[:, None] * frequency[None, :]
    cos = jnp.cos(angles)
    sin = jnp.sin(angles)
    info = jnp.concatenate([count0[None], cache_len, sink_count, base])

    w0, w1 = w_expert[0], w_expert[1]
    wy0 = lax.ppermute(w0, "head", [(0, 1), (1, 0), (2, 3), (3, 2)])
    wy1 = lax.ppermute(w1, "head", [(1, 2), (2, 1), (3, 0), (0, 3)])
    w_oth = swap_core(w_expert)
    wz0 = swap_core(wy0)
    wz1 = swap_core(wy1)
    weights = (w_expert, w_oth, wy0, wy1, wz0, wz1)

    new_k, new_v, *mixed = attention(
        info,
        (own, left, right, far_a, far_b),
        attn_gain[None, :],
        w_qkv.transpose(1, 0, 2),
        jnp.concatenate([cos, cos], axis=1),
        jnp.concatenate([-sin, sin], axis=1),
        cache_k,
        cache_v,
        w_out,
    )
    attended = ring_scatter(*mixed, "y")
    residual = (tokens.astype(F32) + attended).astype(BF)
    wide = residual.astype(F32)
    ffn_input = (
        wide * lax.rsqrt(jnp.mean(wide * wide, axis=-1, keepdims=True) + norm_eps) * ffn_gain
    ).astype(BF)
    lanes = jnp.arange(TAIL, dtype=jnp.int32)
    share = jnp.sum(
        jnp.where(routes[:, :, None] == lanes[None, None, :], route_weight[:, :, None], 0.0), axis=1
    ).astype(BF)
    payload = jnp.concatenate([ffn_input, share], axis=1)
    other = shift(payload, "y", 2)

    line_a = jnp.concatenate(ring_gather(payload, "x"), axis=0)
    line_b = jnp.concatenate(ring_gather(other, "z"), axis=0)
    plane_a = ring_gather(line_a, "z")
    plane_b = ring_gather(line_b, "x")
    chip = tok // 2 * 4
    core = tok % 2 * 2
    ids = jnp.stack([chip + core, chip + core + 1, chip + 2 - core, chip + 3 - core]).astype(
        jnp.int32
    )
    rows = line_a.shape[0]
    near = experts(ids, plane_a[:3] + plane_b[:3], weights, rows, part, "near")
    far = experts(ids, plane_a[3:] + plane_b[3:], weights, rows, part, "far")

    sum_a = ring_scatter(*near[:3], *far[:2], "z").astype(BF)
    sum_b = ring_scatter(*near[3:], *far[2:], "x").astype(BF)

    def cut(v):
        half = part // 2
        return (
            v[:part],
            v[part : 2 * part],
            v[2 * part : 3 * part],
            v[3 * part : 3 * part + half],
            v[3 * part + half :],
        )

    mine = ring_scatter(*cut(sum_a), "x")
    theirs = ring_scatter(*cut(sum_b), "z").astype(BF)
    combined = mine + shift(theirs, "y", 2).astype(F32)
    hidden_out = (residual.astype(F32) + combined).astype(BF)
    return (hidden_out, new_k, new_v)


def solution(mesh):
    return jax.shard_map(
        on_device,
        mesh=mesh,
        in_specs=(
            P(("tok", "head"), None),
            P(("tok", "head")),
            P("tok"),
            P("tok"),
            P("tok", None, "head"),
            P("tok", None, "head"),
            P(),
            P(None, None, "head"),
            P("head", None),
            P(),
            P(("tok", "head"), None),
            P(("tok", "head"), None),
            P("tok", None, None, "head"),
        ),
        out_specs=(P(("tok", "head"), None), P("tok", None, "head"), P("tok", None, "head")),
        check_vma=False,
    )
```

```python
import functools

import jax
import jax.numpy as jnp
from jax import lax
from jax.experimental import pallas as pl
from jax.experimental.pallas import tpu as pltpu
from jax.sharding import PartitionSpec as P


HD = 128
WIN = 384
MOST = 16
norm_eps = 1e-05
rope_base = 50000.0
NX, NZ, NY = 4, 4, 4
BF = jnp.bfloat16
F32 = jnp.float32
TAIL = 128


def tok_perm(move):
    pairs = []
    for x in range(NX):
        for z in range(NZ):
            for c in range(2):
                nx, nz, nc = move(x, z, c)
                pairs.append(((x * NZ + z) * 2 + c, ((nx % NX) * NZ + nz % NZ) * 2 + nc))
    return pairs


def shift(value, axis, step):
    if axis == "y":
        return lax.ppermute(value, "head", [(i, (i + step) % NY) for i in range(NY)])
    if axis == "x":
        return lax.ppermute(value, "tok", tok_perm(lambda x, z, c: (x + step, z, c)))
    return lax.ppermute(value, "tok", tok_perm(lambda x, z, c: (x, z + step, c)))


def swap_core(value):
    return lax.ppermute(value, "tok", tok_perm(lambda x, z, c: (x, z, 1 - c)))


def ring_gather(value, axis):
    half = value.shape[0] // 2
    left = shift(value, axis, 1)
    right = shift(value, axis, -1)
    far_a = shift(left[:half], axis, 1)
    far_b = shift(right[half:], axis, -1)
    return value, left, right, far_a, far_b


def ring_scatter(own, left, right, far_a, far_b, axis):
    got_a = shift(far_a, axis, 1)
    got_b = shift(far_b, axis, -1)
    half = far_a.shape[0]
    got_a = jnp.pad(got_a, ((0, half), (0, 0)))
    got_b = jnp.pad(got_b, ((half, 0), (0, 0)))
    to_right = (right.astype(F32) + got_a.astype(F32)).astype(BF)
    to_left = (left.astype(F32) + got_b.astype(F32)).astype(BF)
    from_left = shift(to_right, axis, 1)
    from_right = shift(to_left, axis, -1)
    return own.astype(F32) + from_left.astype(F32) + from_right.astype(F32)


def short_gather(value, axis):
    return value, shift(value, axis, 1), shift(value, axis, -1), shift(value, axis, 2)


def short_scatter(own, left, right, far, axis):
    from_left = shift(right, axis, 1)
    from_right = shift(left, axis, -1)
    from_far = shift(far, axis, 2)
    return (own.astype(F32) + from_left.astype(F32)) + (
        from_right.astype(F32) + from_far.astype(F32)
    )


def nt_dot(a, b):
    return lax.dot_general(a, b, (((1,), (1,)), ((), ())), preferred_element_type=F32)


def attn_kernel(
    lens,
    sinks_of,
    x0,
    x1,
    x2,
    x3,
    gain,
    freq,
    w3,
    ck,
    cv,
    wo,
    nk,
    nv,
    m0,
    m1,
    m2,
    m3,
    xn,
    hot,
    bias,
    cos,
    sin,
    att,
    count,
    *,
    rows,
    heads,
    cap,
):
    h = pl.program_id(0)
    part = rows // 4
    width = xn.shape[1]
    y = lax.axis_index("head")
    bases = [((y + d) % NY) * part for d in (0, NY - 1, 1, 2)]

    @pl.when(h == 0)
    def _():
        second = sum(jnp.sum(x[:, width:].astype(F32)) for x in (x0, x1, x2, x3))
        count[0] = rows - (second / TAIL).astype(jnp.int32)

    count0, len0, len1 = count[0], lens[0], lens[1]

    def index_of(iota):
        piece = iota // part
        base = jnp.where(
            piece == 0,
            bases[0],
            jnp.where(piece == 1, bases[1], jnp.where(piece == 2, bases[2], bases[3])),
        )
        return base + iota % part

    col = index_of(lax.broadcasted_iota(jnp.int32, (rows, 1), 0))
    first_col = col < count0
    pos_col = jnp.where(first_col, len0 + col, len1 + col - count0)

    @pl.when(h == 0)
    def _():
        xs = jnp.concatenate([x[:, :width] for x in (x0, x1, x2, x3)], axis=0).astype(F32)
        mean = jnp.mean(xs * xs, axis=-1, keepdims=True)
        xn[...] = (xs * lax.rsqrt(mean + norm_eps) * gain[...]).astype(BF)
        row = index_of(lax.broadcasted_iota(jnp.int32, (1, rows), 1))
        first_row = row < count0
        slot_row = jnp.where(first_row, len0 + row, cap + len1 + row - count0)
        slots = lax.broadcasted_iota(jnp.int32, (2 * cap, rows), 0)
        hot[...] = (slots == slot_row).astype(F32).astype(BF)
        j = lax.broadcasted_iota(jnp.int32, (rows, cap), 1)
        sinks = jnp.where(first_col, sinks_of[0], sinks_of[1])
        ok = (j <= pos_col) & ((j < sinks) | (j > pos_col - WIN))
        bias[...] = jnp.where(ok, 0.0, -1e30)
        angles = pos_col.astype(F32) * freq[...]
        cos[...] = jnp.cos(angles)
        lanes = lax.broadcasted_iota(jnp.int32, (rows, HD), 1)
        sin[...] = jnp.sin(angles) * jnp.where(lanes < HD // 2, -1.0, 1.0)

    xv = xn[...]
    q = jnp.dot(xv, w3[0], preferred_element_type=F32)
    k = jnp.dot(xv, w3[1], preferred_element_type=F32)
    v = jnp.dot(xv, w3[2], preferred_element_type=F32)
    c, s = cos[...], sin[...]
    q = (q * c + pltpu.roll(q, HD // 2, 1) * s).astype(BF)
    k = (k * c + pltpu.roll(k, HD // 2, 1) * s).astype(BF)
    kv = jnp.concatenate([k, v.astype(BF)], axis=1)
    slot = lax.broadcasted_iota(jnp.int32, (cap, 1), 0)
    scale = HD**-0.5
    scores = []
    values = []
    for r, start, number in ((0, len0, count0), (1, len1, rows - count0)):
        ins = jnp.dot(hot[r * cap : (r + 1) * cap, :], kv, preferred_element_type=F32)
        fresh = (slot >= start) & (slot < start + number)
        new_k = jnp.where(fresh, ins[:, :HD], ck[r].astype(F32)).astype(BF)
        new_v = jnp.where(fresh, ins[:, HD:], cv[r].astype(F32)).astype(BF)
        nk[r] = new_k
        nv[r] = new_v
        scores.append(nt_dot(q, new_k))
        values.append(new_v)
    masked = jnp.where(first_col, scores[0], scores[1]) * scale + bias[...]
    top = jnp.max(masked, axis=1, keepdims=True)
    weights = jnp.exp(masked - top)
    total = jnp.sum(weights, axis=1, keepdims=True)
    w0 = jnp.where(first_col, weights, 0.0).astype(BF)
    w1 = jnp.where(first_col, 0.0, weights).astype(BF)
    out = jnp.dot(w0, values[0], preferred_element_type=F32) + jnp.dot(
        w1, values[1], preferred_element_type=F32
    )
    att[h] = (out / total).astype(BF)

    @pl.when(h == heads - 1)
    def _():
        both = jnp.concatenate([att[i] for i in range(heads)], axis=1)
        mixed = jnp.dot(both, wo[...], preferred_element_type=F32).astype(BF)
        m0[...] = mixed[:part]
        m1[...] = mixed[part : 2 * part]
        m2[...] = mixed[2 * part : 3 * part]
        m3[...] = mixed[3 * part :]


def attention(lens, sinks, pieces, gain, freq, w3, cache_k, cache_v, w_out):
    part, wide = pieces[0].shape
    width = wide - TAIL
    rows = 4 * part
    reqs, cap, cols = cache_k.shape
    heads = cols // HD
    fixed = lambda *shape: pl.BlockSpec(shape, lambda h: (0,) * len(shape))
    scalars = pl.BlockSpec(memory_space=pltpu.SMEM)
    whole = pl.BlockSpec(memory_space=pltpu.VMEM)
    cache_spec = pl.BlockSpec((reqs, cap, HD), lambda h: (0, 0, h))
    outs = [jax.ShapeDtypeStruct(cache_k.shape, BF)] * 2 + [
        jax.ShapeDtypeStruct((part, width), BF) for _ in pieces
    ]
    return pl.pallas_call(
        functools.partial(attn_kernel, rows=rows, heads=heads, cap=cap),
        out_shape=outs,
        grid=(heads,),
        in_specs=[scalars, scalars]
        + [whole] * len(pieces)
        + [
            fixed(1, width),
            fixed(1, HD),
            pl.BlockSpec((3, width, HD), lambda h: (0, 0, h)),
            cache_spec,
            cache_spec,
            fixed(*w_out.shape),
        ],
        out_specs=[cache_spec, cache_spec] + [whole] * len(pieces),
        scratch_shapes=[
            pltpu.VMEM((rows, width), BF),
            pltpu.VMEM((2 * cap, rows), BF),
            pltpu.VMEM((rows, cap), F32),
            pltpu.VMEM((rows, HD), F32),
            pltpu.VMEM((rows, HD), F32),
            pltpu.VMEM((heads, rows, HD), BF),
            pltpu.SMEM((1,), jnp.int32),
        ],
        compiler_params=pltpu.CompilerParams(vmem_limit_bytes=56 << 20),
        name="attn",
    )(lens, sinks, *pieces, gain, freq, w3, cache_k, cache_v, w_out)


def expert_kernel(*refs, plan, tiles, block, gate):
    n = len(plan)
    xs = refs[:n]
    w_own, w_oth, wy0, wy1, wz0, wz1 = refs[n : n + 6]
    outs = refs[n + 6 + gate : 2 * n + 6 + gate]
    wt, xg, yt, mix, sem_w = refs[2 * n + 6 + gate :]
    tok = lax.axis_index("tok")
    chip = tok // 2 * 4
    core = tok % 2 * 2
    ids = [chip + core, chip + core + 1, chip + 2 - core, chip + 3 - core]
    rows = mix.shape[1]
    width = yt.shape[2]
    blocks = rows // block
    lot = blocks * MOST
    slots = 4 * lot
    held = [[i for i, (tile, _) in enumerate(plan) if tile == t] for t in range(tiles)]

    def tile_of(t, cols):
        return jnp.concatenate([xs[i][:, cols] for i in held[t]], axis=0)

    sources = [
        (w_own.at[0], wy0),
        (w_own.at[1], wy1),
        (w_oth.at[0], wz0),
        (w_oth.at[1], wz1),
    ]
    for e in range(4):
        for s in range(2):
            pltpu.make_async_copy(sources[e][s], wt.at[e, s], sem_w.at[e, s]).start()

    lane = lax.broadcasted_iota(jnp.int32, (TAIL, slots), 0)
    column = lax.broadcasted_iota(jnp.int32, (TAIL, slots), 1)
    which = column // lot
    wanted = jnp.where(
        which == 0, ids[0], jnp.where(which == 1, ids[1], jnp.where(which == 2, ids[2], ids[3]))
    )
    spread = (lane == wanted).astype(F32).astype(BF)
    ti = lax.broadcasted_iota(jnp.int32, (rows, rows), 0)
    tj = lax.broadcasted_iota(jnp.int32, (rows, rows), 1)
    earlier = ((tj < ti) & (ti // block == tj // block)).astype(F32).astype(BF)
    sc = lax.broadcasted_iota(jnp.int32, (rows, slots), 1)
    st = lax.broadcasted_iota(jnp.int32, (rows, slots), 0)
    same_block = (sc // MOST) % blocks == st // block
    slot_of = (sc % MOST).astype(F32)

    for t in range(tiles):
        share = jnp.dot(tile_of(t, slice(width, None)), spread, preferred_element_type=F32)
        taken = (share > 0.0).astype(F32)
        before = jnp.dot(earlier, taken.astype(BF), preferred_element_type=F32)
        here = same_block & (before == slot_of) & (share > 0.0)
        mix[t] = jnp.where(here, share, 0.0).astype(BF)
        picks = here.astype(F32).astype(BF)
        got = lax.dot_general(
            picks, tile_of(t, slice(0, width)), (((0,), (0,)), ((), ())), preferred_element_type=F32
        ).astype(BF)
        for e in range(4):
            xg[e, t * lot : (t + 1) * lot, :] = got[e * lot : (e + 1) * lot]

    step = 512 if width % 512 == 0 else width

    def one_expert(e, carry):
        x = xg[e]
        acts = []
        for s in range(2):
            pltpu.make_async_copy(wy0, wt.at[e, s], sem_w.at[e, s]).wait()
            gate_part = jnp.dot(x, wt[e, s, 0], preferred_element_type=F32)
            up_part = jnp.dot(x, wt[e, s, 1], preferred_element_type=F32)
            acts.append((gate_part / (1.0 + jnp.exp(-gate_part)) * up_part).astype(BF))
        at = pl.multiple_of(e * lot, lot)
        for d in range(0, width, step):
            part = nt_dot(acts[0], wt[e, 0, 2, d : d + step, :]) + nt_dot(
                acts[1], wt[e, 1, 2, d : d + step, :]
            )
            part = part.astype(BF)
            for t in range(tiles):
                yt[t, pl.ds(at, lot), d : d + step] = part[t * lot : (t + 1) * lot]
        return carry

    lax.fori_loop(0, 4, one_expert, 0)

    for t in range(tiles):
        result = jnp.dot(mix[t], yt[t], preferred_element_type=F32).astype(BF)
        for i in held[t]:
            at = plan[i][1]
            outs[i][...] = result[at : at + outs[i].shape[0]]


def experts(pieces, weights, rows, block, after=()):
    plan = []
    at = 0
    for p in pieces:
        plan.append((at // rows, at % rows))
        at += p.shape[0]
    tiles = at // rows
    wide = pieces[0].shape[1]
    width = wide - TAIL
    lot = rows // block * MOST
    n = len(pieces)
    any_spec = pl.BlockSpec(memory_space=pl.ANY)
    near_spec = pl.BlockSpec(memory_space=pltpu.VMEM)
    ff = weights[0].shape[-1]
    return pl.pallas_call(
        functools.partial(
            expert_kernel, plan=tuple(plan), tiles=tiles, block=block, gate=len(after)
        ),
        out_shape=[jax.ShapeDtypeStruct((p.shape[0], width), BF) for p in pieces],
        in_specs=[near_spec] * n + [any_spec] * 6 + [near_spec] * len(after),
        out_specs=[near_spec] * n,
        scratch_shapes=[
            pltpu.VMEM((4, 2, 3, width, ff), BF),
            pltpu.VMEM((4, tiles * lot, width), BF),
            pltpu.VMEM((tiles, 4 * lot, width), BF),
            pltpu.VMEM((tiles, rows, 4 * lot), BF),
            pltpu.SemaphoreType.DMA((4, 2)),
        ],
        compiler_params=pltpu.CompilerParams(vmem_limit_bytes=60 << 20),
    )(*pieces, *weights, *after)


def on_device(
    tokens,
    token_req,
    cache_len,
    sink_count,
    cache_k,
    cache_v,
    attn_gain,
    w_qkv,
    w_out,
    ffn_gain,
    routes,
    route_weight,
    w_expert,
):
    part, _ = tokens.shape

    marks = jnp.broadcast_to(token_req.astype(BF)[:, None], (part, TAIL))
    marked = jnp.concatenate([tokens, marks], axis=1)
    group = short_gather(marked, "y")
    frequency = rope_base ** (-(jnp.arange(HD // 2, dtype=F32) * 2.0 / HD))
    frequency = jnp.concatenate([frequency, frequency])[None, :]

    w0, w1 = w_expert[0], w_expert[1]
    wy0 = lax.ppermute(w0, "head", [(0, 1), (1, 0), (2, 3), (3, 2)])
    wy1 = lax.ppermute(w1, "head", [(1, 2), (2, 1), (3, 0), (0, 3)])
    w_oth = swap_core(w_expert)
    wz0 = swap_core(wy0)
    wz1 = swap_core(wy1)
    weights = (w_expert, w_oth, wy0, wy1, wz0, wz1)

    new_k, new_v, *mixed = attention(
        cache_len,
        sink_count,
        group,
        attn_gain[None, :],
        frequency,
        w_qkv.transpose(1, 0, 2),
        cache_k,
        cache_v,
        w_out,
    )
    attended = short_scatter(*mixed, "y")
    residual = (tokens.astype(F32) + attended).astype(BF)
    wide = residual.astype(F32)
    ffn_input = (
        wide * lax.rsqrt(jnp.mean(wide * wide, axis=-1, keepdims=True) + norm_eps) * ffn_gain
    ).astype(BF)
    lanes = jnp.arange(TAIL, dtype=jnp.int32)
    share = jnp.sum(
        jnp.where(routes[:, :, None] == lanes[None, None, :], route_weight[:, :, None], 0.0), axis=1
    ).astype(BF)
    payload = jnp.concatenate([ffn_input, share], axis=1)
    other = shift(payload, "y", 2)

    line_a = jnp.concatenate(short_gather(payload, "x"), axis=0)
    line_b = jnp.concatenate(short_gather(other, "z"), axis=0)
    plane_a = ring_gather(line_a, "z")
    plane_b = ring_gather(line_b, "x")
    rows = line_a.shape[0]
    near = experts(plane_a[:3] + plane_b[:3], weights, rows, part)
    far = experts(plane_a[3:] + plane_b[3:], weights, rows, part, after=near[:1])

    sum_a = ring_scatter(*near[:3], *far[:2], "z").astype(BF)
    sum_b = ring_scatter(*near[3:], *far[2:], "x").astype(BF)

    def cut(v):
        return v[:part], v[part : 2 * part], v[2 * part : 3 * part], v[3 * part :]

    mine = short_scatter(*cut(sum_a), "x")
    theirs = short_scatter(*cut(sum_b), "z").astype(BF)
    combined = mine + shift(theirs, "y", 2).astype(F32)
    hidden_out = (residual.astype(F32) + combined).astype(BF)
    return (hidden_out, new_k, new_v)


def solution(mesh):
    return jax.shard_map(
        on_device,
        mesh=mesh,
        in_specs=(
            P(("tok", "head"), None),
            P(("tok", "head")),
            P("tok"),
            P("tok"),
            P("tok", None, "head"),
            P("tok", None, "head"),
            P(),
            P(None, None, "head"),
            P("head", None),
            P(),
            P(("tok", "head"), None),
            P(("tok", "head"), None),
            P("tok", None, None, "head"),
        ),
        out_specs=(P(("tok", "head"), None), P("tok", None, "head"), P("tok", None, "head")),
        check_vma=False,
    )
```

```python
import functools

import jax
import jax.numpy as jnp
from jax import lax
from jax.experimental import pallas as pl
from jax.experimental.pallas import tpu as pltpu
from jax.sharding import PartitionSpec as P


HD = 128
WIN = 384
MOST = 16
norm_eps = 1e-05
rope_base = 50000.0
NX, NZ, NY = 4, 4, 4
BF = jnp.bfloat16
F32 = jnp.float32
TAIL = 128


def tok_perm(move):
    pairs = []
    for x in range(NX):
        for z in range(NZ):
            for c in range(2):
                nx, nz, nc = move(x, z, c)
                pairs.append(((x * NZ + z) * 2 + c, ((nx % NX) * NZ + nz % NZ) * 2 + nc))
    return pairs


def shift(value, axis, step):
    if axis == "y":
        return lax.ppermute(value, "head", [(i, (i + step) % NY) for i in range(NY)])
    if axis == "x":
        return lax.ppermute(value, "tok", tok_perm(lambda x, z, c: (x + step, z, c)))
    return lax.ppermute(value, "tok", tok_perm(lambda x, z, c: (x, z + step, c)))


def swap_core(value):
    return lax.ppermute(value, "tok", tok_perm(lambda x, z, c: (x, z, 1 - c)))


def ring_gather(first, second, axis):
    left0 = shift(first, axis, 1)
    right1 = shift(second, axis, -1)
    left1 = shift(second, axis, 1)
    right0 = shift(first, axis, -1)
    far0 = shift(left0, axis, 1)
    far1 = shift(right1, axis, -1)
    return [first, second, left0, left1, right0, right1], [far0, far1]


def plus(a, b):
    return (a.astype(F32) + b.astype(F32)).astype(BF)


def ring_scatter(near, far, axis):
    own0, own1, left0, left1, right0, right1 = near
    from_left1 = shift(right1, axis, 1)
    from_right0 = shift(left0, axis, -1)
    got0 = shift(far[0], axis, 1)
    got1 = shift(far[1], axis, -1)
    from_left0 = shift(plus(right0, got0), axis, 1)
    from_right1 = shift(plus(left1, got1), axis, -1)
    half0 = own0.astype(F32) + from_left0.astype(F32) + from_right0.astype(F32)
    half1 = own1.astype(F32) + from_left1.astype(F32) + from_right1.astype(F32)
    return half0, half1


def short_gather(value, axis):
    return value, shift(value, axis, 1), shift(value, axis, -1), shift(value, axis, 2)


def short_scatter(own, left, right, far, axis):
    from_left = shift(right, axis, 1)
    from_right = shift(left, axis, -1)
    from_far = shift(far, axis, 2)
    return (own.astype(F32) + from_left.astype(F32)) + (
        from_right.astype(F32) + from_far.astype(F32)
    )


def in_vmem(value):
    return pltpu.with_memory_space_constraint(value, pltpu.VMEM)


def nt_dot(a, b):
    return lax.dot_general(a, b, (((1,), (1,)), ((), ())), preferred_element_type=F32)


def attn_kernel(
    lens,
    sinks_of,
    x0,
    x1,
    x2,
    x3,
    gain,
    freq,
    w3,
    ck,
    cv,
    wo,
    nk,
    nv,
    m0,
    m1,
    m2,
    m3,
    xn,
    hot,
    bias,
    cos,
    sin,
    att,
    count,
    *,
    rows,
    heads,
    cap,
):
    h = pl.program_id(0)
    part = rows // 4
    width = xn.shape[1]
    y = lax.axis_index("head")
    bases = [((y + d) % NY) * part for d in (0, NY - 1, 1, 2)]

    @pl.when(h == 0)
    def _():
        second = sum(jnp.sum(x[:, width:].astype(F32)) for x in (x0, x1, x2, x3))
        count[0] = rows - (second / TAIL).astype(jnp.int32)

    count0, len0, len1 = count[0], lens[0], lens[1]

    def index_of(iota):
        piece = iota // part
        base = jnp.where(
            piece == 0,
            bases[0],
            jnp.where(piece == 1, bases[1], jnp.where(piece == 2, bases[2], bases[3])),
        )
        return base + iota % part

    col = index_of(lax.broadcasted_iota(jnp.int32, (rows, 1), 0))
    first_col = col < count0
    pos_col = jnp.where(first_col, len0 + col, len1 + col - count0)

    @pl.when(h == 0)
    def _():
        xs = jnp.concatenate([x[:, :width] for x in (x0, x1, x2, x3)], axis=0).astype(F32)
        mean = jnp.mean(xs * xs, axis=-1, keepdims=True)
        xn[...] = (xs * lax.rsqrt(mean + norm_eps) * gain[...]).astype(BF)
        row = index_of(lax.broadcasted_iota(jnp.int32, (1, rows), 1))
        first_row = row < count0
        slot_row = jnp.where(first_row, len0 + row, cap + len1 + row - count0)
        slots = lax.broadcasted_iota(jnp.int32, (2 * cap, rows), 0)
        hot[...] = (slots == slot_row).astype(F32).astype(BF)
        j = lax.broadcasted_iota(jnp.int32, (rows, cap), 1)
        sinks = jnp.where(first_col, sinks_of[0], sinks_of[1])
        ok = (j <= pos_col) & ((j < sinks) | (j > pos_col - WIN))
        bias[...] = jnp.where(ok, 0.0, -1e30)
        angles = pos_col.astype(F32) * freq[...]
        cos[...] = jnp.cos(angles)
        lanes = lax.broadcasted_iota(jnp.int32, (rows, HD), 1)
        sin[...] = jnp.sin(angles) * jnp.where(lanes < HD // 2, -1.0, 1.0)

    xv = xn[...]
    q = jnp.dot(xv, w3[0], preferred_element_type=F32)
    k = jnp.dot(xv, w3[1], preferred_element_type=F32)
    v = jnp.dot(xv, w3[2], preferred_element_type=F32)
    c, s = cos[...], sin[...]
    q = (q * c + pltpu.roll(q, HD // 2, 1) * s).astype(BF)
    k = (k * c + pltpu.roll(k, HD // 2, 1) * s).astype(BF)
    kv = jnp.concatenate([k, v.astype(BF)], axis=1)
    slot = lax.broadcasted_iota(jnp.int32, (cap, 1), 0)
    scale = HD**-0.5
    scores = []
    values = []
    for r, start, number in ((0, len0, count0), (1, len1, rows - count0)):
        ins = jnp.dot(hot[r * cap : (r + 1) * cap, :], kv, preferred_element_type=F32)
        fresh = (slot >= start) & (slot < start + number)
        new_k = jnp.where(fresh, ins[:, :HD], ck[r].astype(F32)).astype(BF)
        new_v = jnp.where(fresh, ins[:, HD:], cv[r].astype(F32)).astype(BF)
        nk[r] = new_k
        nv[r] = new_v
        scores.append(nt_dot(q, new_k))
        values.append(new_v)
    masked = jnp.where(first_col, scores[0], scores[1]) * scale + bias[...]
    top = jnp.max(masked, axis=1, keepdims=True)
    weights = jnp.exp(masked - top)
    total = jnp.sum(weights, axis=1, keepdims=True)
    w0 = jnp.where(first_col, weights, 0.0).astype(BF)
    w1 = jnp.where(first_col, 0.0, weights).astype(BF)
    out = jnp.dot(w0, values[0], preferred_element_type=F32) + jnp.dot(
        w1, values[1], preferred_element_type=F32
    )
    att[h] = (out / total).astype(BF)

    @pl.when(h == heads - 1)
    def _():
        both = jnp.concatenate([att[i] for i in range(heads)], axis=1)
        mixed = jnp.dot(both, wo[...], preferred_element_type=F32).astype(BF)
        m0[...] = mixed[:part]
        m1[...] = mixed[part : 2 * part]
        m2[...] = mixed[2 * part : 3 * part]
        m3[...] = mixed[3 * part :]


def attention(lens, sinks, pieces, gain, freq, w3, cache_k, cache_v, w_out):
    part, wide = pieces[0].shape
    width = wide - TAIL
    rows = 4 * part
    reqs, cap, cols = cache_k.shape
    heads = cols // HD
    fixed = lambda *shape: pl.BlockSpec(shape, lambda h: (0,) * len(shape))
    scalars = pl.BlockSpec(memory_space=pltpu.SMEM)
    whole = pl.BlockSpec(memory_space=pltpu.VMEM)
    cache_spec = pl.BlockSpec((reqs, cap, HD), lambda h: (0, 0, h))
    outs = [jax.ShapeDtypeStruct(cache_k.shape, BF)] * 2 + [
        pltpu.VMEM((part, width), BF) for _ in pieces
    ]
    return pl.pallas_call(
        functools.partial(attn_kernel, rows=rows, heads=heads, cap=cap),
        out_shape=outs,
        grid=(heads,),
        in_specs=[scalars, scalars]
        + [whole] * len(pieces)
        + [
            fixed(1, width),
            fixed(1, HD),
            pl.BlockSpec((3, width, HD), lambda h: (0, 0, h)),
            cache_spec,
            cache_spec,
            fixed(*w_out.shape),
        ],
        out_specs=[cache_spec, cache_spec] + [whole] * len(pieces),
        scratch_shapes=[
            pltpu.VMEM((rows, width), BF),
            pltpu.VMEM((2 * cap, rows), BF),
            pltpu.VMEM((rows, cap), F32),
            pltpu.VMEM((rows, HD), F32),
            pltpu.VMEM((rows, HD), F32),
            pltpu.VMEM((heads, rows, HD), BF),
            pltpu.SMEM((1,), jnp.int32),
        ],
        compiler_params=pltpu.CompilerParams(vmem_limit_bytes=36 << 20),
        name="attn",
    )(lens, sinks, *map(in_vmem, pieces), gain, freq, w3, cache_k, cache_v, w_out)


def expert_kernel(*refs, plan, tiles, block, gate):
    n = len(plan)
    xs = refs[:n]
    w_own, w_oth = refs[n : n + 2]
    gates, rests = refs[n + 2 : n + 6], refs[n + 6 : n + 10]
    outs = refs[n + 10 + gate : 2 * n + 10 + gate]
    wt, xg, mix, sem_w = refs[2 * n + 10 + gate :]
    tok = lax.axis_index("tok")
    chip = tok // 2 * 4
    core = tok % 2 * 2
    ids = [chip + core, chip + core + 1, chip + 2 - core, chip + 3 - core]
    rows = mix.shape[1]
    width = xg.shape[2]
    blocks = rows // block
    lot = blocks * MOST
    slots = 4 * lot
    held = [[i for i, (tile, _) in enumerate(plan) if tile == t] for t in range(tiles)]

    def tile_of(t, cols):
        return jnp.concatenate([xs[i][:, cols] for i in held[t]], axis=0)

    wholes = [w_own.at[0], w_own.at[1], w_oth.at[0], w_oth.at[1]]
    for e in range(4):
        pltpu.make_async_copy(wholes[e], wt.at[e, 0], sem_w.at[e, 0]).start()
        pltpu.make_async_copy(gates[e], wt.at[e, 1, 0], sem_w.at[e, 1]).start()
        pltpu.make_async_copy(rests[e], wt.at[e, 1, pl.ds(1, 2)], sem_w.at[e, 2]).start()

    lane = lax.broadcasted_iota(jnp.int32, (TAIL, slots), 0)
    column = lax.broadcasted_iota(jnp.int32, (TAIL, slots), 1)
    which = column // lot
    wanted = jnp.where(
        which == 0, ids[0], jnp.where(which == 1, ids[1], jnp.where(which == 2, ids[2], ids[3]))
    )
    spread = (lane == wanted).astype(F32).astype(BF)
    ti = lax.broadcasted_iota(jnp.int32, (rows, rows), 0)
    tj = lax.broadcasted_iota(jnp.int32, (rows, rows), 1)
    earlier = ((tj < ti) & (ti // block == tj // block)).astype(F32).astype(BF)
    sc = lax.broadcasted_iota(jnp.int32, (rows, slots), 1)
    st = lax.broadcasted_iota(jnp.int32, (rows, slots), 0)
    same_block = (sc // MOST) % blocks == st // block
    slot_of = (sc % MOST).astype(F32)

    for t in range(tiles):
        share = jnp.dot(tile_of(t, slice(width, None)), spread, preferred_element_type=F32)
        taken = (share > 0.0).astype(F32)
        before = jnp.dot(earlier, taken.astype(BF), preferred_element_type=F32)
        here = same_block & (before == slot_of) & (share > 0.0)
        mix[t] = jnp.where(here, share, 0.0).astype(BF)
        picks = here.astype(F32).astype(BF)
        got = lax.dot_general(
            picks, tile_of(t, slice(0, width)), (((0,), (0,)), ((), ())), preferred_element_type=F32
        ).astype(BF)
        for e in range(4):
            xg[e, t * lot : (t + 1) * lot, :] = got[e * lot : (e + 1) * lot]

    step = 512 if width % 512 == 0 else width

    def one_expert(e, carry):
        x = xg[e]
        acts = []
        for s in range(2):
            if s == 0:
                pltpu.make_async_copy(wholes[0], wt.at[e, 0], sem_w.at[e, 0]).wait()
            else:
                pltpu.make_async_copy(gates[0], wt.at[e, 1, 0], sem_w.at[e, 1]).wait()
                pltpu.make_async_copy(rests[0], wt.at[e, 1, pl.ds(1, 2)], sem_w.at[e, 2]).wait()
            gate_part = jnp.dot(x, wt[e, s, 0], preferred_element_type=F32)
            up_part = jnp.dot(x, wt[e, s, 1], preferred_element_type=F32)
            acts.append((gate_part / (1.0 + jnp.exp(-gate_part)) * up_part).astype(BF))
        for d in range(0, width, step):
            part = nt_dot(acts[0], wt[e, 0, 2, d : d + step, :]) + nt_dot(
                acts[1], wt[e, 1, 2, d : d + step, :]
            )
            xg[e, :, d : d + step] = part.astype(BF)
        return carry

    lax.fori_loop(0, 4, one_expert, 0)

    for t in range(tiles):
        done = jnp.concatenate([xg[e, t * lot : (t + 1) * lot, :] for e in range(4)], axis=0)
        result = jnp.dot(mix[t], done, preferred_element_type=F32).astype(BF)
        for i in held[t]:
            at = plan[i][1]
            outs[i][...] = result[at : at + outs[i].shape[0]]


def experts(pieces, weights, rows, block, after=()):
    plan = []
    at = 0
    for p in pieces:
        plan.append((at // rows, at % rows))
        at += p.shape[0]
    tiles = at // rows
    wide = pieces[0].shape[1]
    width = wide - TAIL
    lot = rows // block * MOST
    n = len(pieces)
    any_spec = pl.BlockSpec(memory_space=pl.ANY)
    near_spec = pl.BlockSpec(memory_space=pltpu.VMEM)
    ff = weights[0].shape[-1]
    return pl.pallas_call(
        functools.partial(
            expert_kernel, plan=tuple(plan), tiles=tiles, block=block, gate=len(after)
        ),
        out_shape=[pltpu.VMEM((p.shape[0], width), BF) for p in pieces],
        in_specs=[near_spec] * n + [any_spec] * 10 + [near_spec] * len(after),
        out_specs=[near_spec] * n,
        scratch_shapes=[
            pltpu.VMEM((4, 2, 3, width, ff), BF),
            pltpu.VMEM((4, tiles * lot, width), BF),
            pltpu.VMEM((tiles, rows, 4 * lot), BF),
            pltpu.SemaphoreType.DMA((4, 3)),
        ],
        compiler_params=pltpu.CompilerParams(vmem_limit_bytes=(44 if tiles > 2 else 34) << 20),
    )(*map(in_vmem, pieces), *weights, *map(in_vmem, after))


def on_device(
    tokens,
    token_req,
    cache_len,
    sink_count,
    cache_k,
    cache_v,
    attn_gain,
    w_qkv,
    w_out,
    ffn_gain,
    routes,
    route_weight,
    w_expert,
):
    part, _ = tokens.shape

    marks = jnp.broadcast_to(token_req.astype(BF)[:, None], (part, TAIL))
    marked = jnp.concatenate([tokens, marks], axis=1)
    group = short_gather(marked, "y")
    frequency = rope_base ** (-(jnp.arange(HD // 2, dtype=F32) * 2.0 / HD))
    frequency = jnp.concatenate([frequency, frequency])[None, :]

    gate0, gate1 = w_expert[0, 0], w_expert[1, 0]
    rest0, rest1 = w_expert[0, 1:], w_expert[1, 1:]
    pair_a = [(0, 1), (1, 0), (2, 3), (3, 2)]
    pair_b = [(1, 2), (2, 1), (3, 0), (0, 3)]
    gate_y0 = lax.ppermute(gate0, "head", pair_a)
    gate_y1 = lax.ppermute(gate1, "head", pair_b)
    rest_y0 = lax.ppermute(rest0, "head", pair_a)
    rest_y1 = lax.ppermute(rest1, "head", pair_b)
    w_oth = swap_core(w_expert)
    gate_z0 = swap_core(gate_y0)
    gate_z1 = swap_core(gate_y1)
    rest_z0 = swap_core(rest_y0)
    rest_z1 = swap_core(rest_y1)
    weights = (
        w_expert,
        w_oth,
        gate_y0,
        gate_y1,
        gate_z0,
        gate_z1,
        rest_y0,
        rest_y1,
        rest_z0,
        rest_z1,
    )

    new_k, new_v, *mixed = attention(
        cache_len,
        sink_count,
        group,
        attn_gain[None, :],
        frequency,
        w_qkv.transpose(1, 0, 2),
        cache_k,
        cache_v,
        w_out,
    )
    attended = short_scatter(*mixed, "y")
    residual = (tokens.astype(F32) + attended).astype(BF)
    wide = residual.astype(F32)
    ffn_input = (
        wide * lax.rsqrt(jnp.mean(wide * wide, axis=-1, keepdims=True) + norm_eps) * ffn_gain
    ).astype(BF)
    lanes = jnp.arange(TAIL, dtype=jnp.int32)
    share = jnp.sum(
        jnp.where(routes[:, :, None] == lanes[None, None, :], route_weight[:, :, None], 0.0), axis=1
    ).astype(BF)
    payload = jnp.concatenate([ffn_input, share], axis=1)
    other = shift(payload, "y", 2)

    def line(value, axis):
        own, left, right, far = short_gather(value, axis)
        return jnp.concatenate([own, left], axis=0), jnp.concatenate([right, far], axis=0)

    line_a = line(payload, "x")
    line_b = line(other, "z")
    near_a, far_a = ring_gather(*line_a, "z")
    near_b, far_b = ring_gather(*line_b, "x")
    rows = 4 * part
    near = experts(near_a + near_b, weights, rows, part)
    far = experts(far_a + far_b, weights, rows, part, after=near[:1])

    sum_a = ring_scatter(near[:6], far[:2], "z")
    sum_b = ring_scatter(near[6:], far[2:], "x")

    def cut(halves):
        return [v.astype(BF) for h in halves for v in (h[:part], h[part:])]

    mine = short_scatter(*cut(sum_a), "x")
    theirs = short_scatter(*cut(sum_b), "z").astype(BF)
    combined = mine + shift(theirs, "y", 2).astype(F32)
    hidden_out = (residual.astype(F32) + combined).astype(BF)
    return (hidden_out, new_k, new_v)


def solution(mesh):
    return jax.shard_map(
        on_device,
        mesh=mesh,
        in_specs=(
            P(("tok", "head"), None),
            P(("tok", "head")),
            P("tok"),
            P("tok"),
            P("tok", None, "head"),
            P("tok", None, "head"),
            P(),
            P(None, None, "head"),
            P("head", None),
            P(),
            P(("tok", "head"), None),
            P(("tok", "head"), None),
            P("tok", None, None, "head"),
        ),
        out_specs=(P(("tok", "head"), None), P("tok", None, "head"), P("tok", None, "head")),
        check_vma=False,
    )
```
